32 devices in a mesh: mem: 8 (over z, core), dom: 4 (over y, x).
Axes of the slice: x: 2, y: 2, z: 4, core: 2. Of those that a mesh axis runs over, the one named last changes fastest.
Arguments:
- prior_ensemble: float32 [64, 4, 512, 512], P('mem', None, 'dom'), may hold values from -6 to 6
- spreading_factor: float32 [4], replicated, may hold values from 0.05 to 0.24
- tendency_matrix: float32 [4, 4], replicated, may hold values from -0.6 to 0.6
- measured_data: float32 [4, 4096], P('dom', 'mem'), may hold values from -6 to 6
- inverse_error: float32 [4, 4096], P('dom', 'mem'), may hold values from 0.1 to 1
- assigned_subregion: int32 [4, 4096, 1], P('dom', 'mem'), may hold values from 0 to 31; in each aligned block of 512 rows (0 to 511, 512 to 1023, ..., all dimensions but the last counted through in order) at most 32 rows name the same one
- measured_entry: int32 [4, 4096], P('dom', 'mem'), may hold values from 0 to 8191
- taper_index: int32 [4, 4096], P('dom', 'mem'), may hold values from 0 to 63
- taper_factors: float32 [64], replicated, may hold values from 0.2 to 1
Outputs:
- analysis: float32 [64, 4, 512, 512], P('mem', None, 'dom')
The draws below stay inside these ranges and needn't reach their ends.
Inputs may be any that keep to these rules, and one draw needn't show every extreme that they name: `assigned_subregion`: in the rows of one device no patch is named by more than 32 rows, a bound that some block reaches.
All inputs are finite; a program needn't handle non-finite values.
Results may differ from the reference program's by a relative error of at most 0.0003.
Values sent between devices are 32-bit elements; how exact they have to be, the bound alone decides.
A program may use at most 128 MiB of HBM per device.

```python
import math
import jax
import jax.numpy as jnp
import numpy as np
from jax import lax

ENSEMBLE_SIZE = 64
PROGNOSTIC_VARS = 4
PATCH = 2048
SUBDOMAIN_LINES = 128
EAST_WEST_SPAN = 512
OBS_DEV = 512
NS_ITERS = 5
LOC_LEVELS = 64
NORTH_SOUTH_SPAN = 512
PATCH_TILE = 32
OBS_CAP = 32
OBS_TILE = 4096
N_DOM = 4


def plant(entries, own_key, smallest, high):
    shape = entries.shape
    place = [jax.random.randint(jax.random.fold_in(own_key, axis), (), 0, shape[axis]) for axis in range(len(shape))]
    entries = entries.at[tuple(place)].set(smallest)
    longest = shape.index(max(shape))
    place[longest] = (place[longest] + 1) % shape[longest]
    return entries.at[tuple(place)].set(high)


def block_levels(rng, extent, cuts, least, top_value):
    def one(dim, blocks):
        draws = jax.random.uniform(jax.random.fold_in(jax.random.fold_in(rng, 6), dim), (blocks,), jnp.float32, least / len(cuts), top_value / len(cuts))
        return jnp.repeat(jnp.exp(draws), extent[dim] // blocks).reshape((-1,) + (1,) * (len(extent) - dim - 1))

    gain = one(*cuts[0])
    for cut in cuts[1:]:
        gain = gain * one(*cut)
    return gain


def deal_out(key, own, number, rows, number_of, top, bound, slope):
    sequence = jax.random.permutation(key, number_of)
    packed, common = portions_of(number_of, rows * top, bound, slope, True), portions_of(number_of, rows * top, bound, slope, False)
    places = jnp.arange(number_of)

    def named(tallies, offset_by):
        used = int((tallies > 0).sum())
        fixed = max(1, used // 4)
        passed = fixed + (places - fixed + offset_by * (used - fixed)) % max(1, number_of - fixed)
        return jnp.zeros((number_of,), jnp.int32).at[sequence[jnp.where(places < fixed, places, passed)]].set(jnp.asarray(tallies, jnp.int32))

    tallies = jnp.where(number % 4 == 0, named(packed, number // 4), named(common, number - number // 4 - 1))
    mixed = jax.random.permutation(jax.random.fold_in(own, 3), number_of)
    giver, sink = mixed[0:number_of // 2 * 2:2], mixed[1:number_of // 2 * 2:2]
    margin = jnp.minimum(tallies[giver] - 1, bound - tallies[sink]) // 2
    margin = jnp.where((giver == sequence[0]) | (sink == sequence[0]) | (tallies[sink] == 0), 0, jnp.maximum(margin, 0))
    passed = jax.random.randint(jax.random.fold_in(own, 4), (number_of // 2,), 0, 1 << 20) % (margin + 1)
    tallies = tallies.at[giver].add(-passed).at[sink].add(passed)
    members = jnp.searchsorted(jnp.cumsum(tallies), jnp.arange(rows * top), side="right").astype(jnp.int32)
    table = members.reshape(top, rows).T
    table = table[jax.random.permutation(jax.random.fold_in(own, 1), rows)]
    offset_by = jax.random.randint(jax.random.fold_in(own, 2), (rows, 1), 0, top)
    return jnp.take_along_axis(table, (jnp.arange(top)[None, :] + offset_by) % top, axis=1)


def portions_of(number_of, total, limit, slope, full):
    loads = [(1 << 20) // math.isqrt(grade ** slope) + 1 for grade in range(1, number_of + 1)]
    largest = limit if full else min(limit, max(-(-total // number_of), total * loads[0] // sum(loads)))
    least = 1 if total - largest >= number_of - 1 else 0
    holding, spare = [largest] + [least] * (number_of - 1), total - largest - least * (number_of - 1)
    while spare > 0:
        movable = [i for i in range(1, number_of) if holding[i] < largest] or [i for i in range(1, number_of) if holding[i] < limit]
        whole, remaining = sum([loads[i] for i in movable]), spare
        for i in movable:
            extra = min(limit - holding[i], max(1, remaining * loads[i] // whole), spare)
            holding[i] = holding[i] + extra
            spare = spare - extra
    return np.array(holding)


def noise(rng, dims, spread, limit, pieces=(), kind=jnp.bfloat16):
    entries = spread * jax.random.normal(rng, dims, jnp.float32)
    if pieces:
        entries = entries * block_levels(rng, dims, pieces, -0.22, 0.18)
    return jnp.clip(entries, -limit, limit).astype(kind)


def setup_inputs(seed: int = 0) -> dict:
    seeds = jax.random.split(jax.random.key(seed), 10)
    prior_ensemble = noise(seeds[0], (ENSEMBLE_SIZE, PROGNOSTIC_VARS, NORTH_SOUTH_SPAN, EAST_WEST_SPAN), 1.0, 6.0, ((0, 8), (2, 4)), jnp.float32)
    spreading_factor = jnp.clip(jnp.exp(jax.random.uniform(seeds[1], (PROGNOSTIC_VARS,), jnp.float32, math.log(0.05), math.log(0.24))), 0.05, 0.24)
    tendency_matrix = noise(seeds[2], (PROGNOSTIC_VARS, PROGNOSTIC_VARS), 0.15, 0.6, (), jnp.float32)
    measured_data = noise(seeds[3], (N_DOM, OBS_TILE), 1.0, 6.0, ((0, 4), (1, 8)), jnp.float32)
    inverse_error = jnp.clip(jnp.exp(math.log(1.0) - 2.3025851 * jax.random.uniform(seeds[4], (N_DOM, OBS_TILE), jnp.float32) ** block_levels(seeds[4], (N_DOM, OBS_TILE), ((0, 4), (1, 8)), -0.2, 0.2)), 0.1, 1.0)
    assigned_subregion_keys = jax.random.split(jax.random.fold_in(seeds[5], 1), N_DOM * OBS_TILE // OBS_DEV)
    assigned_subregion_turns = jax.random.permutation(jax.random.fold_in(seeds[5], 3), N_DOM * OBS_TILE // OBS_DEV)
    assigned_subregion = jax.vmap(lambda own, number: deal_out(jax.random.fold_in(seeds[5], 2), own, number, OBS_DEV, PATCH_TILE, 1, OBS_CAP, 2))(assigned_subregion_keys, assigned_subregion_turns).reshape((N_DOM, OBS_TILE, 1))
    measured_entry = plant(jax.random.randint(seeds[6], (N_DOM, OBS_TILE), 0, PROGNOSTIC_VARS * PATCH), jax.random.fold_in(seeds[6], 1), 0, (PROGNOSTIC_VARS * PATCH) - 1).astype(jnp.int32)
    taper_index = plant(jax.random.randint(seeds[7], (N_DOM, OBS_TILE), 0, LOC_LEVELS), jax.random.fold_in(seeds[7], 1), 0, LOC_LEVELS - 1).astype(jnp.int32)
    taper_factors = jnp.clip(jnp.exp(jax.random.uniform(seeds[8], (LOC_LEVELS,), jnp.float32, math.log(0.2), math.log(1.0))), 0.2, 1.0)
    return {"prior_ensemble": prior_ensemble, "spreading_factor": spreading_factor, "tendency_matrix": tendency_matrix, "measured_data": measured_data, "inverse_error": inverse_error, "assigned_subregion": assigned_subregion, "measured_entry": measured_entry, "taper_index": taper_index, "taper_factors": taper_factors}


HIGH = lax.Precision.HIGHEST

def laplacian_update(haloed_ensemble, ensemble, spreading_factor, tendency_matrix):
    subdomain_lines = ensemble.shape[2]
    beside = jnp.pad(ensemble, ((0, 0), (0, 0), (0, 0), (1, 1)))
    laplace = haloed_ensemble[:, :, 2:] + haloed_ensemble[:, :, :subdomain_lines] + beside[:, :, :, 2:] + beside[:, :, :, :-2] - 4.0 * ensemble
    mixing = jnp.einsum('vw,kwxy->kvxy', tendency_matrix, ensemble, precision=HIGH)
    return ensemble + spreading_factor[None, :, None, None] * laplace + mixing

def transforms(gram, drive, member_count):
    identity_m = jnp.eye(member_count, dtype=jnp.float32)
    system = (member_count - 1.0) * identity_m + gram
    norm_value = jnp.sqrt(lax.optimization_barrier(jnp.sum(system * system, axis=(-2, -1))))
    iterate = system / norm_value[..., None, None]
    inverse = jnp.broadcast_to(identity_m, system.shape)
    for sweep_no in range(NS_ITERS):
        middle = 1.5 * identity_m - 0.5 * jnp.einsum('...ij,...jk->...ik', inverse, iterate, precision=HIGH)
        iterate = jnp.einsum('...ij,...jk->...ik', iterate, middle, precision=HIGH)
        inverse = jnp.einsum('...ij,...jk->...ik', middle, inverse, precision=HIGH)
    root = inverse / jnp.sqrt(norm_value)[..., None, None]
    inner = jnp.einsum('...ij,...j->...i', root, drive, precision=HIGH)
    offset = jnp.einsum('...ij,...j->...i', root, inner, precision=HIGH)
    return offset[..., :, None] + jnp.sqrt(member_count - 1.0) * root

def reference(prior_ensemble, spreading_factor, tendency_matrix, measured_data, inverse_error, assigned_subregion, measured_entry, taper_index, taper_factors):
    subdomain_number = prior_ensemble.reshape(ENSEMBLE_SIZE, PROGNOSTIC_VARS, N_DOM, SUBDOMAIN_LINES, EAST_WEST_SPAN)
    blank = jnp.zeros((ENSEMBLE_SIZE, PROGNOSTIC_VARS, 1, EAST_WEST_SPAN), jnp.float32)
    last_rows = subdomain_number[:, :, :, SUBDOMAIN_LINES - 1, :]
    first_rows = subdomain_number[:, :, :, 0, :]
    below_all = jnp.concatenate([blank, last_rows[:, :, :-1]], axis=2)
    above_all = jnp.concatenate([first_rows[:, :, 1:], blank], axis=2)
    weights_all = inverse_error * taper_factors[taper_index]

    def one_tile(tile_index):
        block = lax.dynamic_index_in_dim(subdomain_number, tile_index, 2, keepdims=False)
        below = lax.dynamic_slice_in_dim(below_all, tile_index, 1, 2)
        above = lax.dynamic_slice_in_dim(above_all, tile_index, 1, 2)
        haloed_ensemble = jnp.concatenate([below, block, above], axis=2)
        advanced_ensemble = laplacian_update(haloed_ensemble, block, spreading_factor, tendency_matrix).reshape(ENSEMBLE_SIZE, PROGNOSTIC_VARS, PATCH_TILE, PATCH)
        tile_patch = lax.dynamic_index_in_dim(assigned_subregion, tile_index, 0, keepdims=False)[:, 0]
        tile_cell = lax.dynamic_index_in_dim(measured_entry, tile_index, 0, keepdims=False)
        tile_value = lax.dynamic_index_in_dim(measured_data, tile_index, 0, keepdims=False)
        tile_weight = lax.dynamic_index_in_dim(weights_all, tile_index, 0, keepdims=False)

        def one_patch(patch_index):
            ensemble = lax.dynamic_index_in_dim(advanced_ensemble, patch_index, 2, keepdims=False).reshape(ENSEMBLE_SIZE, PROGNOSTIC_VARS * PATCH)
            centre = lax.optimization_barrier(jnp.mean(ensemble, axis=0))
            deviation = ensemble - centre[None]
            chosen = jnp.where(tile_patch == patch_index, tile_weight, jnp.zeros_like(tile_weight))
            columns = jnp.take(deviation, tile_cell, axis=1)
            innovation = tile_value - jnp.take(centre, tile_cell)
            weighted = columns * chosen[None]
            gram = jnp.dot(weighted, columns.T, precision=HIGH)
            drive = jnp.dot(weighted, innovation, precision=HIGH)
            coeffs = transforms(gram, drive, ENSEMBLE_SIZE)
            return centre[None] + jnp.dot(coeffs.T, deviation, precision=HIGH)
        done = lax.map(one_patch, jnp.arange(PATCH_TILE, dtype=jnp.int32))
        return done.reshape(PATCH_TILE, ENSEMBLE_SIZE, PROGNOSTIC_VARS, PATCH).transpose(1, 2, 0, 3).reshape(ENSEMBLE_SIZE, PROGNOSTIC_VARS, SUBDOMAIN_LINES, EAST_WEST_SPAN)
    result = lax.map(one_tile, jnp.arange(N_DOM, dtype=jnp.int32))
    return result.transpose(1, 2, 0, 3, 4).reshape(ENSEMBLE_SIZE, PROGNOSTIC_VARS, N_DOM * SUBDOMAIN_LINES, EAST_WEST_SPAN)
```

```python
import functools

import jax
import jax.numpy as jnp
from jax import lax
from jax.experimental import pallas as pl
from jax.experimental.pallas import tpu as pltpu
from jax.sharding import PartitionSpec as P

PATCH = 2048
NS_ITERS = 5


HIGH = lax.Precision.HIGHEST


def padded(block, sides, width):
    for axis, dim in sides:
        count = lax.axis_size(axis)
        forward = [(i, i + 1) for i in range(count - 1)]
        backward = [(target, source) for source, target in forward]
        low = lax.ppermute(
            lax.slice_in_dim(block, block.shape[dim] - width, None, axis=dim), axis, forward
        )
        high = lax.ppermute(lax.slice_in_dim(block, 0, width, axis=dim), axis, backward)
        block = jnp.concatenate([low, block, high], axis=dim)
    return block


def laplacian_update(haloed_ensemble, ensemble, spreading_factor, tendency_matrix):
    subdomain_lines = ensemble.shape[2]
    beside = jnp.pad(ensemble, ((0, 0), (0, 0), (0, 0), (1, 1)))
    laplace = (
        haloed_ensemble[:, :, 2:]
        + haloed_ensemble[:, :, :subdomain_lines]
        + beside[:, :, :, 2:]
        + beside[:, :, :, :-2]
        - 4.0 * ensemble
    )
    mixing = jnp.einsum("vw,kwxy->kvxy", tendency_matrix, ensemble, precision=HIGH)
    return ensemble + spreading_factor[None, :, None, None] * laplace + mixing


def transforms(gram, drive, member_count):
    identity_m = jnp.eye(member_count, dtype=jnp.float32)
    system = (member_count - 1.0) * identity_m + gram
    norm_value = jnp.sqrt(jnp.sum(system * system, axis=(-2, -1)))
    iterate = system / norm_value[..., None, None]
    inverse = jnp.broadcast_to(identity_m, system.shape)
    for sweep_no in range(NS_ITERS):
        middle = 1.5 * identity_m - 0.5 * jnp.einsum(
            "...ij,...jk->...ik", inverse, iterate, precision=HIGH
        )
        iterate = jnp.einsum("...ij,...jk->...ik", iterate, middle, precision=HIGH)
        inverse = jnp.einsum("...ij,...jk->...ik", middle, inverse, precision=HIGH)
    root = inverse / jnp.sqrt(norm_value)[..., None, None]
    inner = jnp.einsum("...ij,...j->...i", root, drive, precision=HIGH)
    offset = jnp.einsum("...ij,...j->...i", root, inner, precision=HIGH)
    return offset[..., :, None] + jnp.sqrt(member_count - 1.0) * root


def slot_ranks(patch_ids, patch_count):
    onehot = (patch_ids[..., None] == jnp.arange(patch_count, dtype=jnp.int32)).astype(jnp.int32)
    before = jnp.cumsum(onehot, axis=-2) - onehot
    return jnp.sum(before * onehot, axis=-1)


def shards(
    prior_ensemble,
    spreading_factor,
    tendency_matrix,
    measured_data,
    inverse_error,
    assigned_subregion,
    measured_entry,
    taper_index,
    taper_factors,
):
    ensemble_share, prognostic_number, subdomain_lines, eastward_span = prior_ensemble.shape
    groups = lax.axis_size("mem")
    members = ensemble_share * groups
    cells_dev = subdomain_lines * eastward_span // groups
    per_device = cells_dev // PATCH
    per_tile = per_device * groups
    haloed_ensemble = padded(prior_ensemble, (("dom", 2),), 1)
    advanced_ensemble = laplacian_update(
        haloed_ensemble, prior_ensemble, spreading_factor, tendency_matrix
    )
    moved = lax.all_to_all(
        advanced_ensemble.reshape(ensemble_share, prognostic_number, groups, cells_dev),
        "mem",
        split_axis=2,
        concat_axis=0,
        tiled=True,
    )
    ensemble = moved.reshape(members, prognostic_number, cells_dev)
    patch_ids = assigned_subregion.reshape(-1)
    obs_rows = patch_ids.shape[0]
    capacity = 2 * obs_rows // per_tile
    table_levels = taper_factors.shape[0]
    picks = (
        taper_index.reshape(-1)[:, None] == jnp.arange(table_levels, dtype=jnp.int32)[None, :]
    ).astype(jnp.float32)
    weight = inverse_error.reshape(-1) * jnp.dot(picks, taper_factors, precision=HIGH)
    values = measured_data.reshape(-1)
    columns = measured_entry.reshape(-1).astype(jnp.float32)
    target = patch_ids * capacity + slot_ranks(patch_ids, per_tile)

    def place_rows(field):
        return (
            jnp.zeros((per_tile * capacity,), jnp.float32)
            .at[target]
            .set(field)
            .reshape(groups, per_device * capacity)
        )

    received = (
        lax.all_to_all(place_rows(values), "mem", split_axis=0, concat_axis=0, tiled=True),
        lax.all_to_all(place_rows(weight), "mem", split_axis=0, concat_axis=0, tiled=True),
        lax.all_to_all(place_rows(columns), "mem", split_axis=0, concat_axis=0, tiled=True),
    )

    def arrange(field):
        return (
            field.reshape(groups, per_device, capacity)
            .transpose(1, 0, 2)
            .reshape(per_device, groups * capacity)
        )

    slot_value = arrange(received[0])
    slot_weight = arrange(received[1])
    slot_column = arrange(received[2])
    centre = jnp.mean(ensemble, axis=0)
    deviation = ensemble - centre[None]
    column_ids = slot_column.astype(jnp.int32)
    flat_index = (
        column_ids // PATCH * cells_dev
        + jnp.arange(per_device, dtype=jnp.int32)[:, None] * PATCH
        + column_ids % PATCH
    )
    flat_index = flat_index.reshape(-1)
    flat_dev = deviation.reshape(members, prognostic_number * cells_dev)
    obs_dev = jnp.take(flat_dev, flat_index, axis=1).reshape(members, per_device, -1)
    innovation = slot_value - jnp.take(centre.reshape(-1), flat_index).reshape(per_device, -1)
    weighted = obs_dev * slot_weight[None]
    gram = jnp.einsum("kps,jps->pkj", weighted, obs_dev, precision=HIGH)
    drive = jnp.einsum("kps,ps->pk", weighted, innovation, precision=HIGH)
    coeffs = transforms(gram, drive, members)
    dev_blocks = deviation.reshape(members, prognostic_number, per_device, PATCH)
    mixed = jnp.einsum("pjk,jvpt->kvpt", coeffs, dev_blocks, precision=HIGH)
    analysed = centre.reshape(1, prognostic_number, per_device, PATCH) + mixed
    outgoing = analysed.reshape(groups, ensemble_share, prognostic_number, cells_dev)
    returned = lax.all_to_all(outgoing, "mem", split_axis=0, concat_axis=3, tiled=True)
    return returned.reshape(ensemble_share, prognostic_number, subdomain_lines, eastward_span)


LANES = 128


def split3(field):
    high = field.astype(jnp.bfloat16)
    rest = field - high.astype(jnp.float32)
    middle = rest.astype(jnp.bfloat16)
    low = (rest - middle.astype(jnp.float32)).astype(jnp.bfloat16)
    return [high, middle, low]


def dot(a, b, dims=((1,), (0,))):
    return lax.dot_general(
        a, b, (dims, ((), ())), precision=HIGH, preferred_element_type=jnp.float32
    )


def analysis_kernel(
    groups, tiles, per_device, patch_lines, lanes_own,
    factor, tendency, state, obs, result,
    field, outbox, inbox, answer, obs_in, dev, centre, picked,
    load_sem, halo_send, halo_recv, obs_send, obs_recv, obs_own,
    go_send, go_recv, go_own, back_send, back_recv, back_own,
):
    mine = lax.axis_index("mem")
    tile = lax.axis_index("dom")
    variables, lines, share, span = state.shape
    members = groups * share
    device_lines = per_device * patch_lines
    chunks = variables * patch_lines
    order = sorted(range(1, groups), key=lambda t: abs(t - groups // 2))
    upper = lax.rem(tile + 1, tiles)
    lower = lax.rem(tile + tiles - 1, tiles)

    load = pltpu.make_async_copy(state, field.at[:, pl.ds(1, lines)], load_sem)
    load.start()

    barrier = pltpu.get_barrier_semaphore()
    for t in range(1, groups):
        pl.semaphore_signal(barrier, 1, device_id={"mem": lax.rem(mine + t, groups)})
    for other in (upper, lower):
        pl.semaphore_signal(barrier, 1, device_id={"dom": other})
    pl.semaphore_wait(barrier, groups + 1)

    halos = []
    for side, (line, place, other) in enumerate(((lines - 1, 0, upper), (0, lines + 1, lower))):
        halos.append(
            pltpu.make_async_remote_copy(
                src_ref=state.at[:, pl.ds(line, 1)],
                dst_ref=field.at[:, pl.ds(place, 1)],
                send_sem=halo_send.at[side],
                recv_sem=halo_recv.at[side],
                device_id={"dom": other},
            )
        )
        halos[-1].start()

    def obs_copy(t):
        to = lax.rem(mine + t, groups)
        return pltpu.make_async_remote_copy(
            src_ref=obs.at[to],
            dst_ref=obs_in.at[mine],
            send_sem=obs_send.at[t],
            recv_sem=obs_recv.at[t],
            device_id={"mem": to},
        )

    def go_copy(p, t):
        to = lax.rem(mine + t, groups)
        return pltpu.make_async_remote_copy(
            src_ref=outbox.at[to, p],
            dst_ref=inbox.at[p, mine],
            send_sem=go_send.at[p, t],
            recv_sem=go_recv.at[p, t],
            device_id={"mem": to},
        )

    def go_local(p):
        return pltpu.make_async_copy(outbox.at[mine, p], inbox.at[p, mine], go_own.at[p])

    def result_lines(p):
        return result.at[:, pl.ds(mine * device_lines + p * patch_lines, patch_lines)]

    def back_copy(p, t):
        to = lax.rem(mine + t, groups)
        return pltpu.make_async_remote_copy(
            src_ref=answer.at[p, to],
            dst_ref=result_lines(p),
            send_sem=back_send.at[p, t],
            recv_sem=back_recv.at[p, t],
            device_id={"mem": to},
        )

    def back_local(p):
        return pltpu.make_async_copy(answer.at[p, mine], result_lines(p), back_own.at[p])

    for t in range(1, groups):
        obs_copy(t).start()
    keep = pltpu.make_async_copy(obs.at[mine], obs_in.at[mine], obs_own)
    keep.start()

    load.wait()
    for copy in halos:
        copy.wait()
    for place, outside in ((0, tile == 0), (lines + 1, tile == tiles - 1)):
        for v in range(variables):
            field[v, place] = jnp.where(outside, 0.0, field[v, place])

    lane = lax.broadcasted_iota(jnp.int32, (share, span), 1)

    def advance(p, to):
        def one_line(r, carry):
            line = to * device_lines + p * patch_lines + r
            here = [field[w, line + 1] for w in range(variables)]
            for v in range(variables):
                own = here[v]
                west = jnp.where(lane == 0, 0.0, pltpu.roll(own, 1, 1))
                east = jnp.where(lane == span - 1, 0.0, pltpu.roll(own, span - 1, 1))
                laplace = field[v, line + 2] + field[v, line] + east + west - 4.0 * own
                total = own + factor[v] * laplace
                for w in range(variables):
                    total += tendency[v, w] * here[w]
                outbox[to, p, v, r] = total
            return carry

        lax.fori_loop(0, patch_lines, one_line, 0)

    def forecast(p, carry):
        for t in order:
            advance(p, lax.rem(mine + t, groups))
            go_copy(p, t).start()
        advance(p, mine)
        go_local(p).start()
        return carry

    lax.fori_loop(0, per_device, forecast, 0)

    for t in range(1, groups):
        obs_copy(t).wait()
    keep.wait()

    slots = -(-groups // lanes_own) * LANES
    rows_i = lax.broadcasted_iota(jnp.int32, (members, members), 0)
    cols_i = lax.broadcasted_iota(jnp.int32, (members, members), 1)
    identity = jnp.where(rows_i == cols_i, 1.0, 0.0)
    cell = lax.broadcasted_iota(jnp.int32, (span, slots), 0)

    def analyse(p, carry):
        packs = []
        for first in range(0, groups, lanes_own):
            pack = obs_in[first, p]
            for s in range(first + 1, min(first + lanes_own, groups)):
                pack += obs_in[s, p]
            packs.append(pack)
        pack = jnp.concatenate(packs, axis=1)
        value, weight = pack[0:1], pack[1:2]
        column = pack[2:3].astype(jnp.int32)
        picked[...] = jnp.zeros_like(picked)
        for t in range(1, groups):
            go_copy(p, t).wait_recv()
        go_local(p).wait()

        def gather(c, carry):
            v, r = c // patch_lines, c % patch_lines
            block = inbox[p, :, v, r].reshape(members, span)
            mean = jnp.sum(block, axis=0, keepdims=True) * (1.0 / members)
            away = block - mean
            dev[c] = away
            wide = jnp.broadcast_to(mean, (16, span))
            centre[c] = wide[:8]
            parts = jnp.concatenate(split3(away) + split3(wide), axis=0)
            chosen = jnp.where(cell == column - c * span, 1.0, 0.0).astype(jnp.bfloat16)
            picked[...] += jnp.dot(parts, chosen, preferred_element_type=jnp.float32)
            return carry

        lax.fori_loop(0, chunks, gather, 0)
        seen = picked[0:members] + picked[members : 2 * members] + picked[2 * members : 3 * members]
        low = 3 * members
        middle_seen = picked[low : low + 8] + picked[low + 16 : low + 24] + picked[low + 32 : low + 40]
        innovation = value - middle_seen
        weighted = seen * weight
        gram = dot(weighted, seen, ((1,), (1,)))
        drive = jnp.sum(weighted * innovation[0:1], axis=1, keepdims=True)
        system = (members - 1.0) * identity + gram
        squares = jnp.sum(system * system, axis=1, keepdims=True)
        norm = jnp.sqrt(jnp.sum(squares, axis=0, keepdims=True))

        def sweep(i, pair):
            middle = 1.5 * identity - 0.5 * dot(pair[:, members:], pair[:, :members])
            return dot(middle, pair)

        start = jnp.concatenate([system / norm, identity], axis=1)
        pair = start
        for i in range(NS_ITERS):
            pair = sweep(i, pair)
        inverse = pair[:, members:]
        root = inverse / jnp.sqrt(norm)
        inner = jnp.sum(root * drive, axis=0, keepdims=True)
        offset = jnp.sum(root * inner, axis=1, keepdims=True)
        offset = jnp.sum(identity * offset, axis=0, keepdims=True)
        coeffs = offset + float(members - 1) ** 0.5 * root

        def mix(c, carry):
            v, r = c // patch_lines, c % patch_lines
            mixed = dot(coeffs, dev[c]) + centre[c, 0:1]
            answer[p, :, v, r] = mixed.reshape(groups, share, span)
            return carry

        lax.fori_loop(0, chunks, mix, 0)
        for t in order:
            back_copy(p, t).start()
        back_local(p).start()
        return carry

    lax.fori_loop(0, per_device, analyse, 0)

    def finish(p, carry):
        for t in range(1, groups):
            go_copy(p, t).wait_send()
        for t in range(1, groups):
            back_copy(p, t).wait()
        back_local(p).wait()
        return carry

    lax.fori_loop(0, per_device, finish, 0)


def fused(
    prior_ensemble,
    spreading_factor,
    tendency_matrix,
    measured_data,
    inverse_error,
    assigned_subregion,
    measured_entry,
    taper_index,
    taper_factors,
):
    share, variables, lines, span = prior_ensemble.shape
    groups, tiles = lax.axis_size("mem"), lax.axis_size("dom")
    patch_lines = PATCH // span
    per_device = lines // groups // patch_lines
    per_tile = per_device * groups
    members = share * groups
    patch_ids = assigned_subregion.reshape(-1)
    obs_rows = patch_ids.shape[0]
    capacity = 2 * obs_rows // per_tile
    lanes_own = LANES // capacity
    levels = jnp.arange(taper_factors.shape[0], dtype=jnp.int32)
    taper = jnp.sum(
        jnp.where(taper_index.reshape(-1)[:, None] == levels[None], taper_factors[None], 0.0), axis=1
    )
    weight = inverse_error.reshape(-1) * taper
    number = jnp.arange(obs_rows, dtype=jnp.int32)
    rank = jnp.sum(
        ((patch_ids[None, :] == patch_ids[:, None]) & (number[None, :] < number[:, None])).astype(jnp.int32),
        axis=1,
    )
    slot = lax.rem(lax.axis_index("mem"), lanes_own) * capacity + rank
    nothing = jnp.zeros_like(weight)
    fields = jnp.stack(
        [measured_data.reshape(-1), weight, measured_entry.reshape(-1).astype(jnp.float32)]
        + [nothing] * 5
    )
    patches = jnp.arange(per_tile, dtype=jnp.int32)
    spread = jnp.where(patch_ids[None, None] == patches[:, None, None], fields[None], 0.0)
    places = (slot[:, None] == jnp.arange(LANES, dtype=jnp.int32)[None]).astype(jnp.float32)
    obs = jnp.dot(spread.reshape(per_tile * 8, obs_rows), places, precision=HIGH)
    obs = obs.reshape(groups, per_device, 8, LANES)
    state = prior_ensemble.transpose(1, 2, 0, 3)
    chunks = variables * patch_lines
    slots = -(-groups // lanes_own) * LANES
    dma = pltpu.SemaphoreType.DMA
    result = pl.pallas_call(
        functools.partial(analysis_kernel, groups, tiles, per_device, patch_lines, lanes_own),
        out_shape=jax.ShapeDtypeStruct(state.shape, jnp.float32),
        in_specs=[
            pl.BlockSpec(memory_space=pltpu.SMEM),
            pl.BlockSpec(memory_space=pltpu.SMEM),
            pl.BlockSpec(memory_space=pl.ANY),
            pl.BlockSpec(memory_space=pltpu.VMEM),
        ],
        out_specs=pl.BlockSpec(memory_space=pl.ANY),
        scratch_shapes=[
            pltpu.VMEM((variables, lines + 2, share, span), jnp.float32),
            pltpu.VMEM((groups, per_device, variables, patch_lines, share, span), jnp.float32),
            pltpu.VMEM((per_device, groups, variables, patch_lines, share, span), jnp.float32),
            pltpu.VMEM((per_device, groups, variables, patch_lines, share, span), jnp.float32),
            pltpu.VMEM((groups, per_device, 8, LANES), jnp.float32),
            pltpu.VMEM((chunks, members, span), jnp.float32),
            pltpu.VMEM((chunks, 8, span), jnp.float32),
            pltpu.VMEM((3 * members + 48, slots), jnp.float32),
            dma, dma((2,)), dma((2,)), dma((groups,)), dma((groups,)), dma,
            dma((per_device, groups)), dma((per_device, groups)), dma((per_device,)),
            dma((per_device, groups)), dma((per_device, groups)), dma((per_device,)),
        ],
        compiler_params=pltpu.CompilerParams(
            collective_id=0, has_side_effects=True, vmem_limit_bytes=60 * 1024 * 1024
        ),
    )(spreading_factor, tendency_matrix, state, obs)
    return result.transpose(2, 0, 1, 3)


def step(prior_ensemble, *rest):
    share, _, lines, span = prior_ensemble.shape
    groups, tiles = lax.axis_size("mem"), lax.axis_size("dom")
    whole_lines = PATCH % span == 0 and lines % (groups * (PATCH // span)) == 0
    obs_rows = rest[2].shape[-1]
    capacity = 2 * obs_rows * PATCH // (lines * span)
    if share % 8 == 0 and whole_lines and tiles > 1 and groups > 1 and LANES % capacity == 0:
        return fused(prior_ensemble, *rest)
    return shards(prior_ensemble, *rest)


def solution(mesh):
    in_specs = (
        P("mem", None, "dom", None),
        P(),
        P(),
        P("dom", "mem"),
        P("dom", "mem"),
        P("dom", "mem", None),
        P("dom", "mem"),
        P("dom", "mem"),
        P(),
    )
    out_specs = P("mem", None, "dom", None)
    return jax.shard_map(step, mesh=mesh, in_specs=in_specs, out_specs=out_specs, check_vma=False)
```

```python
import functools

import jax
import jax.numpy as jnp
from jax import lax
from jax.experimental import pallas as pl
from jax.experimental.pallas import tpu as pltpu
from jax.sharding import PartitionSpec as P

PATCH = 2048
NS_ITERS = 5


HIGH = lax.Precision.HIGHEST


def padded(block, sides, width):
    for axis, dim in sides:
        count = lax.axis_size(axis)
        forward = [(i, i + 1) for i in range(count - 1)]
        backward = [(target, source) for source, target in forward]
        low = lax.ppermute(
            lax.slice_in_dim(block, block.shape[dim] - width, None, axis=dim), axis, forward
        )
        high = lax.ppermute(lax.slice_in_dim(block, 0, width, axis=dim), axis, backward)
        block = jnp.concatenate([low, block, high], axis=dim)
    return block


def laplacian_update(haloed_ensemble, ensemble, spreading_factor, tendency_matrix):
    subdomain_lines = ensemble.shape[2]
    beside = jnp.pad(ensemble, ((0, 0), (0, 0), (0, 0), (1, 1)))
    laplace = (
        haloed_ensemble[:, :, 2:]
        + haloed_ensemble[:, :, :subdomain_lines]
        + beside[:, :, :, 2:]
        + beside[:, :, :, :-2]
        - 4.0 * ensemble
    )
    mixing = jnp.einsum("vw,kwxy->kvxy", tendency_matrix, ensemble, precision=HIGH)
    return ensemble + spreading_factor[None, :, None, None] * laplace + mixing


def transforms(gram, drive, member_count):
    identity_m = jnp.eye(member_count, dtype=jnp.float32)
    system = (member_count - 1.0) * identity_m + gram
    norm_value = jnp.sqrt(jnp.sum(system * system, axis=(-2, -1)))
    iterate = system / norm_value[..., None, None]
    inverse = jnp.broadcast_to(identity_m, system.shape)
    for sweep_no in range(NS_ITERS):
        middle = 1.5 * identity_m - 0.5 * jnp.einsum(
            "...ij,...jk->...ik", inverse, iterate, precision=HIGH
        )
        iterate = jnp.einsum("...ij,...jk->...ik", iterate, middle, precision=HIGH)
        inverse = jnp.einsum("...ij,...jk->...ik", middle, inverse, precision=HIGH)
    root = inverse / jnp.sqrt(norm_value)[..., None, None]
    inner = jnp.einsum("...ij,...j->...i", root, drive, precision=HIGH)
    offset = jnp.einsum("...ij,...j->...i", root, inner, precision=HIGH)
    return offset[..., :, None] + jnp.sqrt(member_count - 1.0) * root


def slot_ranks(patch_ids, patch_count):
    onehot = (patch_ids[..., None] == jnp.arange(patch_count, dtype=jnp.int32)).astype(jnp.int32)
    before = jnp.cumsum(onehot, axis=-2) - onehot
    return jnp.sum(before * onehot, axis=-1)


def shards(
    prior_ensemble,
    spreading_factor,
    tendency_matrix,
    measured_data,
    inverse_error,
    assigned_subregion,
    measured_entry,
    taper_index,
    taper_factors,
):
    ensemble_share, prognostic_number, subdomain_lines, eastward_span = prior_ensemble.shape
    groups = lax.axis_size("mem")
    members = ensemble_share * groups
    cells_dev = subdomain_lines * eastward_span // groups
    per_device = cells_dev // PATCH
    per_tile = per_device * groups
    haloed_ensemble = padded(prior_ensemble, (("dom", 2),), 1)
    advanced_ensemble = laplacian_update(
        haloed_ensemble, prior_ensemble, spreading_factor, tendency_matrix
    )
    moved = lax.all_to_all(
        advanced_ensemble.reshape(ensemble_share, prognostic_number, groups, cells_dev),
        "mem",
        split_axis=2,
        concat_axis=0,
        tiled=True,
    )
    ensemble = moved.reshape(members, prognostic_number, cells_dev)
    patch_ids = assigned_subregion.reshape(-1)
    obs_rows = patch_ids.shape[0]
    capacity = 2 * obs_rows // per_tile
    table_levels = taper_factors.shape[0]
    picks = (
        taper_index.reshape(-1)[:, None] == jnp.arange(table_levels, dtype=jnp.int32)[None, :]
    ).astype(jnp.float32)
    weight = inverse_error.reshape(-1) * jnp.dot(picks, taper_factors, precision=HIGH)
    values = measured_data.reshape(-1)
    columns = measured_entry.reshape(-1).astype(jnp.float32)
    target = patch_ids * capacity + slot_ranks(patch_ids, per_tile)

    def place_rows(field):
        return (
            jnp.zeros((per_tile * capacity,), jnp.float32)
            .at[target]
            .set(field)
            .reshape(groups, per_device * capacity)
        )

    received = (
        lax.all_to_all(place_rows(values), "mem", split_axis=0, concat_axis=0, tiled=True),
        lax.all_to_all(place_rows(weight), "mem", split_axis=0, concat_axis=0, tiled=True),
        lax.all_to_all(place_rows(columns), "mem", split_axis=0, concat_axis=0, tiled=True),
    )

    def arrange(field):
        return (
            field.reshape(groups, per_device, capacity)
            .transpose(1, 0, 2)
            .reshape(per_device, groups * capacity)
        )

    slot_value = arrange(received[0])
    slot_weight = arrange(received[1])
    slot_column = arrange(received[2])
    centre = jnp.mean(ensemble, axis=0)
    deviation = ensemble - centre[None]
    column_ids = slot_column.astype(jnp.int32)
    flat_index = (
        column_ids // PATCH * cells_dev
        + jnp.arange(per_device, dtype=jnp.int32)[:, None] * PATCH
        + column_ids % PATCH
    )
    flat_index = flat_index.reshape(-1)
    flat_dev = deviation.reshape(members, prognostic_number * cells_dev)
    obs_dev = jnp.take(flat_dev, flat_index, axis=1).reshape(members, per_device, -1)
    innovation = slot_value - jnp.take(centre.reshape(-1), flat_index).reshape(per_device, -1)
    weighted = obs_dev * slot_weight[None]
    gram = jnp.einsum("kps,jps->pkj", weighted, obs_dev, precision=HIGH)
    drive = jnp.einsum("kps,ps->pk", weighted, innovation, precision=HIGH)
    coeffs = transforms(gram, drive, members)
    dev_blocks = deviation.reshape(members, prognostic_number, per_device, PATCH)
    mixed = jnp.einsum("pjk,jvpt->kvpt", coeffs, dev_blocks, precision=HIGH)
    analysed = centre.reshape(1, prognostic_number, per_device, PATCH) + mixed
    outgoing = analysed.reshape(groups, ensemble_share, prognostic_number, cells_dev)
    returned = lax.all_to_all(outgoing, "mem", split_axis=0, concat_axis=3, tiled=True)
    return returned.reshape(ensemble_share, prognostic_number, subdomain_lines, eastward_span)


LANES = 128


def split3(field):
    high = field.astype(jnp.bfloat16)
    rest = field - high.astype(jnp.float32)
    middle = rest.astype(jnp.bfloat16)
    low = (rest - middle.astype(jnp.float32)).astype(jnp.bfloat16)
    return [high, middle, low]


def dot(a, b, dims=((1,), (0,))):
    return lax.dot_general(
        a, b, (dims, ((), ())), precision=HIGH, preferred_element_type=jnp.float32
    )


def analysis_kernel(
    groups, tiles, per_device, patch_lines, lanes_own,
    factor, tendency, state, edges, obs, result,
    raw, field, outbox, inbox, answer, obs_in, dev, centre, picked,
    load_sem, halo_send, halo_recv, obs_send, obs_recv, obs_own,
    go_send, go_recv, go_own, back_send, back_recv, back_own,
):
    mine = lax.axis_index("mem")
    tile = lax.axis_index("dom")
    share, variables, lines, span = state.shape
    members = groups * share
    device_lines = per_device * patch_lines
    chunks = variables * patch_lines
    order = sorted(range(1, groups), key=lambda t: abs(t - groups // 2))
    upper = lax.rem(tile + 1, tiles)
    lower = lax.rem(tile + tiles - 1, tiles)

    parts = 4
    part_lines = lines // parts

    def load(q):
        rows = pl.ds(q * part_lines, part_lines)
        return pltpu.make_async_copy(
            state.at[:, :, rows], raw.at[:, :, rows], load_sem.at[q]
        )

    for q in range(parts):
        load(q).start()

    barrier = pltpu.get_barrier_semaphore()
    for t in range(1, groups):
        pl.semaphore_signal(barrier, 1, device_id={"mem": lax.rem(mine + t, groups)})
    for other in (upper, lower):
        pl.semaphore_signal(barrier, 1, device_id={"dom": other})
    pl.semaphore_wait(barrier, groups + 1)

    halos = []
    for side, (place, other) in enumerate(((0, upper), (lines + 1, lower))):
        halos.append(
            pltpu.make_async_remote_copy(
                src_ref=edges.at[side],
                dst_ref=field.at[:, pl.ds(place, 1)],
                send_sem=halo_send.at[side],
                recv_sem=halo_recv.at[side],
                device_id={"dom": other},
            )
        )
        halos[-1].start()

    def obs_copy(t):
        to = lax.rem(mine + t, groups)
        return pltpu.make_async_remote_copy(
            src_ref=obs.at[to],
            dst_ref=obs_in.at[mine],
            send_sem=obs_send.at[t],
            recv_sem=obs_recv.at[t],
            device_id={"mem": to},
        )

    def go_copy(p, t):
        to = lax.rem(mine + t, groups)
        return pltpu.make_async_remote_copy(
            src_ref=outbox.at[to, p],
            dst_ref=inbox.at[p, mine],
            send_sem=go_send.at[p, t],
            recv_sem=go_recv.at[p, t],
            device_id={"mem": to},
        )

    def go_local(p):
        return pltpu.make_async_copy(outbox.at[mine, p], inbox.at[p, mine], go_own.at[p])

    def result_lines(p):
        return result.at[:, pl.ds(mine * device_lines + p * patch_lines, patch_lines)]

    def back_copy(p, t):
        to = lax.rem(mine + t, groups)
        return pltpu.make_async_remote_copy(
            src_ref=answer.at[p, to],
            dst_ref=result_lines(p),
            send_sem=back_send.at[p, t],
            recv_sem=back_recv.at[p, t],
            device_id={"mem": to},
        )

    def back_local(p):
        return pltpu.make_async_copy(answer.at[p, mine], result_lines(p), back_own.at[p])

    for t in range(1, groups):
        obs_copy(t).start()
    keep = pltpu.make_async_copy(obs.at[mine], obs_in.at[mine], obs_own)
    keep.start()

    for q in range(parts):
        load(q).wait()

        def turn(b, carry, q=q):
            row = pl.multiple_of(q * part_lines + b * 8, 8)
            for v in range(variables):
                block = raw[:, v, pl.ds(row, 8)]
                field[v, pl.ds(row + 1, 8)] = jnp.swapaxes(block, 0, 1)
            return carry

        lax.fori_loop(0, part_lines // 8, turn, 0)
    for copy in halos:
        copy.wait()
    for place, outside in ((0, tile == 0), (lines + 1, tile == tiles - 1)):
        for v in range(variables):
            field[v, place] = jnp.where(outside, 0.0, field[v, place])

    lane = lax.broadcasted_iota(jnp.int32, (share, span), 1)

    def advance(p, to):
        def one_line(r, carry):
            line = to * device_lines + p * patch_lines + r
            here = [field[w, line + 1] for w in range(variables)]
            for v in range(variables):
                own = here[v]
                west = jnp.where(lane == 0, 0.0, pltpu.roll(own, 1, 1))
                east = jnp.where(lane == span - 1, 0.0, pltpu.roll(own, span - 1, 1))
                laplace = field[v, line + 2] + field[v, line] + east + west - 4.0 * own
                total = own + factor[v] * laplace
                for w in range(variables):
                    total += tendency[v, w] * here[w]
                outbox[to, p, v, r] = total
            return carry

        lax.fori_loop(0, patch_lines, one_line, 0)

    def forecast(p, carry):
        for t in order:
            advance(p, lax.rem(mine + t, groups))
            go_copy(p, t).start()
        advance(p, mine)
        go_local(p).start()
        return carry

    lax.fori_loop(0, per_device, forecast, 0)

    for t in range(1, groups):
        obs_copy(t).wait()
    keep.wait()

    slots = -(-groups // lanes_own) * LANES
    rows_i = lax.broadcasted_iota(jnp.int32, (members, members), 0)
    cols_i = lax.broadcasted_iota(jnp.int32, (members, members), 1)
    identity = jnp.where(rows_i == cols_i, 1.0, 0.0)
    cell = lax.broadcasted_iota(jnp.int32, (span, slots), 0)

    def analyse(p, carry):
        packs = []
        for first in range(0, groups, lanes_own):
            pack = obs_in[first, p]
            for s in range(first + 1, min(first + lanes_own, groups)):
                pack += obs_in[s, p]
            packs.append(pack)
        pack = jnp.concatenate(packs, axis=1)
        value, weight = pack[0:1], pack[1:2]
        column = pack[2:3].astype(jnp.int32)
        picked[...] = jnp.zeros_like(picked)
        for t in range(1, groups):
            go_copy(p, t).wait_recv()
        go_local(p).wait()

        def gather(c, carry):
            v, r = c // patch_lines, c % patch_lines
            block = inbox[p, :, v, r].reshape(members, span)
            mean = jnp.sum(block, axis=0, keepdims=True) * (1.0 / members)
            away = block - mean
            dev[c] = away
            wide = jnp.broadcast_to(mean, (16, span))
            centre[c] = wide[:8]
            parts = jnp.concatenate(split3(away) + split3(wide), axis=0)
            chosen = jnp.where(cell == column - c * span, 1.0, 0.0).astype(jnp.bfloat16)
            picked[...] += jnp.dot(parts, chosen, preferred_element_type=jnp.float32)
            return carry

        lax.fori_loop(0, chunks, gather, 0)
        seen = picked[0:members] + picked[members : 2 * members] + picked[2 * members : 3 * members]
        low = 3 * members
        middle_seen = picked[low : low + 8] + picked[low + 16 : low + 24] + picked[low + 32 : low + 40]
        innovation = value - middle_seen
        weighted = seen * weight
        gram = dot(weighted, seen, ((1,), (1,)))
        drive = jnp.sum(weighted * innovation[0:1], axis=1, keepdims=True)
        system = (members - 1.0) * identity + gram
        squares = jnp.sum(system * system, axis=1, keepdims=True)
        norm = jnp.sqrt(jnp.sum(squares, axis=0, keepdims=True))

        def sweep(i, pair):
            middle = 1.5 * identity - 0.5 * dot(pair[:, members:], pair[:, :members])
            return dot(middle, pair)

        start = jnp.concatenate([system / norm, identity], axis=1)
        pair = start
        for i in range(NS_ITERS):
            pair = sweep(i, pair)
        inverse = pair[:, members:]
        root = inverse / jnp.sqrt(norm)
        inner = jnp.sum(root * drive, axis=0, keepdims=True)
        offset = jnp.sum(root * inner, axis=1, keepdims=True)
        offset = jnp.sum(identity * offset, axis=0, keepdims=True)
        coeffs = offset + float(members - 1) ** 0.5 * root

        def mix(c, carry):
            v, r = c // patch_lines, c % patch_lines
            mixed = dot(coeffs, dev[c]) + centre[c, 0:1]
            answer[p, :, v, r] = mixed.reshape(groups, share, span)
            return carry

        lax.fori_loop(0, chunks, mix, 0)
        for t in order:
            back_copy(p, t).start()
        back_local(p).start()
        return carry

    lax.fori_loop(0, per_device, analyse, 0)

    def finish(p, carry):
        for t in range(1, groups):
            go_copy(p, t).wait_send()
        for t in range(1, groups):
            back_copy(p, t).wait()
        back_local(p).wait()
        return carry

    lax.fori_loop(0, per_device, finish, 0)


def turn_kernel(lines_first, members_out):
    for r in range(0, lines_first.shape[1], 8):
        members_out[:, 0, r : r + 8] = jnp.swapaxes(lines_first[0, r : r + 8], 0, 1)


def members_first(result):
    variables, lines, share, span = result.shape
    block = 32
    return pl.pallas_call(
        turn_kernel,
        out_shape=jax.ShapeDtypeStruct((share, variables, lines, span), jnp.float32),
        grid=(variables, lines // block),
        in_specs=[pl.BlockSpec((1, block, share, span), lambda v, b: (v, b, 0, 0))],
        out_specs=pl.BlockSpec((share, 1, block, span), lambda v, b: (0, v, b, 0)),
    )(result)


def fused(
    prior_ensemble,
    spreading_factor,
    tendency_matrix,
    measured_data,
    inverse_error,
    assigned_subregion,
    measured_entry,
    taper_index,
    taper_factors,
):
    share, variables, lines, span = prior_ensemble.shape
    groups, tiles = lax.axis_size("mem"), lax.axis_size("dom")
    patch_lines = PATCH // span
    per_device = lines // groups // patch_lines
    per_tile = per_device * groups
    members = share * groups
    patch_ids = assigned_subregion.reshape(-1)
    obs_rows = patch_ids.shape[0]
    capacity = 2 * obs_rows // per_tile
    lanes_own = LANES // capacity
    levels = jnp.arange(taper_factors.shape[0], dtype=jnp.int32)
    taper = jnp.sum(
        jnp.where(taper_index.reshape(-1)[:, None] == levels[None], taper_factors[None], 0.0), axis=1
    )
    weight = inverse_error.reshape(-1) * taper
    number = jnp.arange(obs_rows, dtype=jnp.int32)
    rank = jnp.sum(
        ((patch_ids[None, :] == patch_ids[:, None]) & (number[None, :] < number[:, None])).astype(jnp.int32),
        axis=1,
    )
    slot = lax.rem(lax.axis_index("mem"), lanes_own) * capacity + rank
    nothing = jnp.zeros_like(weight)
    fields = jnp.stack(
        [measured_data.reshape(-1), weight, measured_entry.reshape(-1).astype(jnp.float32)]
        + [nothing] * 5
    )
    patches = jnp.arange(per_tile, dtype=jnp.int32)
    spread = jnp.where(patch_ids[None, None] == patches[:, None, None], fields[None], 0.0)
    places = (slot[:, None] == jnp.arange(LANES, dtype=jnp.int32)[None]).astype(jnp.float32)
    obs = jnp.dot(spread.reshape(per_tile * 8, obs_rows), places, precision=HIGH)
    obs = obs.reshape(groups, per_device, 8, LANES)
    edges = jnp.stack([prior_ensemble[:, :, -1], prior_ensemble[:, :, 0]])
    edges = edges.transpose(0, 2, 1, 3)[:, :, None]
    chunks = variables * patch_lines
    slots = -(-groups // lanes_own) * LANES
    dma = pltpu.SemaphoreType.DMA
    result = pl.pallas_call(
        functools.partial(analysis_kernel, groups, tiles, per_device, patch_lines, lanes_own),
        out_shape=jax.ShapeDtypeStruct((variables, lines, share, span), jnp.float32),
        in_specs=[
            pl.BlockSpec(memory_space=pltpu.SMEM),
            pl.BlockSpec(memory_space=pltpu.SMEM),
            pl.BlockSpec(memory_space=pl.ANY),
            pl.BlockSpec(memory_space=pltpu.VMEM),
            pl.BlockSpec(memory_space=pltpu.VMEM),
        ],
        out_specs=pl.BlockSpec(memory_space=pl.ANY),
        scratch_shapes=[
            pltpu.VMEM((share, variables, lines, span), jnp.float32),
            pltpu.VMEM((variables, lines + 2, share, span), jnp.float32),
            pltpu.VMEM((groups, per_device, variables, patch_lines, share, span), jnp.float32),
            pltpu.VMEM((per_device, groups, variables, patch_lines, share, span), jnp.float32),
            pltpu.VMEM((per_device, groups, variables, patch_lines, share, span), jnp.float32),
            pltpu.VMEM((groups, per_device, 8, LANES), jnp.float32),
            pltpu.VMEM((chunks, members, span), jnp.float32),
            pltpu.VMEM((chunks, 8, span), jnp.float32),
            pltpu.VMEM((3 * members + 48, slots), jnp.float32),
            dma((4,)), dma((2,)), dma((2,)), dma((groups,)), dma((groups,)), dma,
            dma((per_device, groups)), dma((per_device, groups)), dma((per_device,)),
            dma((per_device, groups)), dma((per_device, groups)), dma((per_device,)),
        ],
        compiler_params=pltpu.CompilerParams(
            collective_id=0, has_side_effects=True, vmem_limit_bytes=60 * 1024 * 1024
        ),
    )(spreading_factor, tendency_matrix, prior_ensemble, edges, obs)
    return members_first(result)


def step(prior_ensemble, *rest):
    share, _, lines, span = prior_ensemble.shape
    groups, tiles = lax.axis_size("mem"), lax.axis_size("dom")
    whole_lines = PATCH % span == 0 and lines % (groups * (PATCH // span)) == 0
    obs_rows = rest[2].shape[-1]
    capacity = 2 * obs_rows * PATCH // (lines * span)
    if share % 8 == 0 and whole_lines and lines % 32 == 0 and tiles > 1 and groups > 1 and LANES % capacity == 0:
        return fused(prior_ensemble, *rest)
    return shards(prior_ensemble, *rest)


def solution(mesh):
    in_specs = (
        P("mem", None, "dom", None),
        P(),
        P(),
        P("dom", "mem"),
        P("dom", "mem"),
        P("dom", "mem", None),
        P("dom", "mem"),
        P("dom", "mem"),
        P(),
    )
    out_specs = P("mem", None, "dom", None)
    return jax.shard_map(step, mesh=mesh, in_specs=in_specs, out_specs=out_specs, check_vma=False)
```

```python
import functools

import jax
import jax.numpy as jnp
from jax import lax
from jax.experimental import pallas as pl
from jax.experimental.pallas import tpu as pltpu
from jax.sharding import PartitionSpec as P

PATCH = 2048
NS_ITERS = 5


HIGH = lax.Precision.HIGHEST


def padded(block, sides, width):
    for axis, dim in sides:
        count = lax.axis_size(axis)
        forward = [(i, i + 1) for i in range(count - 1)]
        backward = [(target, source) for source, target in forward]
        low = lax.ppermute(
            lax.slice_in_dim(block, block.shape[dim] - width, None, axis=dim), axis, forward
        )
        high = lax.ppermute(lax.slice_in_dim(block, 0, width, axis=dim), axis, backward)
        block = jnp.concatenate([low, block, high], axis=dim)
    return block


def laplacian_update(haloed_ensemble, ensemble, spreading_factor, tendency_matrix):
    subdomain_lines = ensemble.shape[2]
    beside = jnp.pad(ensemble, ((0, 0), (0, 0), (0, 0), (1, 1)))
    laplace = (
        haloed_ensemble[:, :, 2:]
        + haloed_ensemble[:, :, :subdomain_lines]
        + beside[:, :, :, 2:]
        + beside[:, :, :, :-2]
        - 4.0 * ensemble
    )
    mixing = jnp.einsum("vw,kwxy->kvxy", tendency_matrix, ensemble, precision=HIGH)
    return ensemble + spreading_factor[None, :, None, None] * laplace + mixing


def transforms(gram, drive, member_count):
    identity_m = jnp.eye(member_count, dtype=jnp.float32)
    system = (member_count - 1.0) * identity_m + gram
    norm_value = jnp.sqrt(jnp.sum(system * system, axis=(-2, -1)))
    iterate = system / norm_value[..., None, None]
    inverse = jnp.broadcast_to(identity_m, system.shape)
    for sweep_no in range(NS_ITERS):
        middle = 1.5 * identity_m - 0.5 * jnp.einsum(
            "...ij,...jk->...ik", inverse, iterate, precision=HIGH
        )
        iterate = jnp.einsum("...ij,...jk->...ik", iterate, middle, precision=HIGH)
        inverse = jnp.einsum("...ij,...jk->...ik", middle, inverse, precision=HIGH)
    root = inverse / jnp.sqrt(norm_value)[..., None, None]
    inner = jnp.einsum("...ij,...j->...i", root, drive, precision=HIGH)
    offset = jnp.einsum("...ij,...j->...i", root, inner, precision=HIGH)
    return offset[..., :, None] + jnp.sqrt(member_count - 1.0) * root


def slot_ranks(patch_ids, patch_count):
    onehot = (patch_ids[..., None] == jnp.arange(patch_count, dtype=jnp.int32)).astype(jnp.int32)
    before = jnp.cumsum(onehot, axis=-2) - onehot
    return jnp.sum(before * onehot, axis=-1)


def shards(
    prior_ensemble,
    spreading_factor,
    tendency_matrix,
    measured_data,
    inverse_error,
    assigned_subregion,
    measured_entry,
    taper_index,
    taper_factors,
):
    ensemble_share, prognostic_number, subdomain_lines, eastward_span = prior_ensemble.shape
    groups = lax.axis_size("mem")
    members = ensemble_share * groups
    cells_dev = subdomain_lines * eastward_span // groups
    per_device = cells_dev // PATCH
    per_tile = per_device * groups
    haloed_ensemble = padded(prior_ensemble, (("dom", 2),), 1)
    advanced_ensemble = laplacian_update(
        haloed_ensemble, prior_ensemble, spreading_factor, tendency_matrix
    )
    moved = lax.all_to_all(
        advanced_ensemble.reshape(ensemble_share, prognostic_number, groups, cells_dev),
        "mem",
        split_axis=2,
        concat_axis=0,
        tiled=True,
    )
    ensemble = moved.reshape(members, prognostic_number, cells_dev)
    patch_ids = assigned_subregion.reshape(-1)
    obs_rows = patch_ids.shape[0]
    capacity = 2 * obs_rows // per_tile
    table_levels = taper_factors.shape[0]
    picks = (
        taper_index.reshape(-1)[:, None] == jnp.arange(table_levels, dtype=jnp.int32)[None, :]
    ).astype(jnp.float32)
    weight = inverse_error.reshape(-1) * jnp.dot(picks, taper_factors, precision=HIGH)
    values = measured_data.reshape(-1)
    columns = measured_entry.reshape(-1).astype(jnp.float32)
    target = patch_ids * capacity + slot_ranks(patch_ids, per_tile)

    def place_rows(field):
        return (
            jnp.zeros((per_tile * capacity,), jnp.float32)
            .at[target]
            .set(field)
            .reshape(groups, per_device * capacity)
        )

    received = (
        lax.all_to_all(place_rows(values), "mem", split_axis=0, concat_axis=0, tiled=True),
        lax.all_to_all(place_rows(weight), "mem", split_axis=0, concat_axis=0, tiled=True),
        lax.all_to_all(place_rows(columns), "mem", split_axis=0, concat_axis=0, tiled=True),
    )

    def arrange(field):
        return (
            field.reshape(groups, per_device, capacity)
            .transpose(1, 0, 2)
            .reshape(per_device, groups * capacity)
        )

    slot_value = arrange(received[0])
    slot_weight = arrange(received[1])
    slot_column = arrange(received[2])
    centre = jnp.mean(ensemble, axis=0)
    deviation = ensemble - centre[None]
    column_ids = slot_column.astype(jnp.int32)
    flat_index = (
        column_ids // PATCH * cells_dev
        + jnp.arange(per_device, dtype=jnp.int32)[:, None] * PATCH
        + column_ids % PATCH
    )
    flat_index = flat_index.reshape(-1)
    flat_dev = deviation.reshape(members, prognostic_number * cells_dev)
    obs_dev = jnp.take(flat_dev, flat_index, axis=1).reshape(members, per_device, -1)
    innovation = slot_value - jnp.take(centre.reshape(-1), flat_index).reshape(per_device, -1)
    weighted = obs_dev * slot_weight[None]
    gram = jnp.einsum("kps,jps->pkj", weighted, obs_dev, precision=HIGH)
    drive = jnp.einsum("kps,ps->pk", weighted, innovation, precision=HIGH)
    coeffs = transforms(gram, drive, members)
    dev_blocks = deviation.reshape(members, prognostic_number, per_device, PATCH)
    mixed = jnp.einsum("pjk,jvpt->kvpt", coeffs, dev_blocks, precision=HIGH)
    analysed = centre.reshape(1, prognostic_number, per_device, PATCH) + mixed
    outgoing = analysed.reshape(groups, ensemble_share, prognostic_number, cells_dev)
    returned = lax.all_to_all(outgoing, "mem", split_axis=0, concat_axis=3, tiled=True)
    return returned.reshape(ensemble_share, prognostic_number, subdomain_lines, eastward_span)


LANES = 128


def split3(field):
    high = field.astype(jnp.bfloat16)
    rest = field - high.astype(jnp.float32)
    middle = rest.astype(jnp.bfloat16)
    low = (rest - middle.astype(jnp.float32)).astype(jnp.bfloat16)
    return [high, middle, low]


def dot(a, b, dims=((1,), (0,))):
    return lax.dot_general(
        a, b, (dims, ((), ())), precision=HIGH, preferred_element_type=jnp.float32
    )


def analysis_kernel(
    groups, tiles, per_device, patch_lines, lanes_own,
    factor, tendency, state, obs, result,
    raw, field, outbox, inbox, answer, obs_in, dev, centre, picked,
    load_sem, halo_send, halo_recv, obs_send, obs_recv, obs_own,
    go_send, go_recv, go_own, back_send, back_recv, back_own,
):
    mine = lax.axis_index("mem")
    tile = lax.axis_index("dom")
    share, variables, lines, span = state.shape
    members = groups * share
    device_lines = per_device * patch_lines
    chunks = variables * patch_lines
    order = sorted(range(1, groups), key=lambda t: abs(t - groups // 2))
    upper = lax.rem(tile + 1, tiles)
    lower = lax.rem(tile + tiles - 1, tiles)

    parts = 4
    part_lines = lines // parts

    def load(q):
        rows = pl.ds(q * part_lines, part_lines)
        return pltpu.make_async_copy(
            state.at[:, :, rows], raw.at[:, :, rows], load_sem.at[q]
        )

    turns = (0, parts - 1) + tuple(range(1, parts - 1))
    for q in turns:
        load(q).start()

    barrier = pltpu.get_barrier_semaphore()
    for t in range(1, groups):
        pl.semaphore_signal(barrier, 1, device_id={"mem": lax.rem(mine + t, groups)})
    for other in (upper, lower):
        pl.semaphore_signal(barrier, 1, device_id={"dom": other})
    pl.semaphore_wait(barrier, groups + 1)

    halos = []
    for side, (line, place, other) in enumerate(((lines, 0, upper), (1, lines + 1, lower))):
        halos.append(
            pltpu.make_async_remote_copy(
                src_ref=field.at[:, pl.ds(line, 1)],
                dst_ref=field.at[:, pl.ds(place, 1)],
                send_sem=halo_send.at[side],
                recv_sem=halo_recv.at[side],
                device_id={"dom": other},
            )
        )

    def obs_copy(t):
        to = lax.rem(mine + t, groups)
        return pltpu.make_async_remote_copy(
            src_ref=obs.at[to],
            dst_ref=obs_in.at[mine],
            send_sem=obs_send.at[t],
            recv_sem=obs_recv.at[t],
            device_id={"mem": to},
        )

    def go_copy(p, t):
        to = lax.rem(mine + t, groups)
        return pltpu.make_async_remote_copy(
            src_ref=outbox.at[to, p],
            dst_ref=inbox.at[p, mine],
            send_sem=go_send.at[p, t],
            recv_sem=go_recv.at[p, t],
            device_id={"mem": to},
        )

    def go_local(p):
        return pltpu.make_async_copy(outbox.at[mine, p], inbox.at[p, mine], go_own.at[p])

    def result_lines(p):
        return result.at[:, pl.ds(mine * device_lines + p * patch_lines, patch_lines)]

    def back_copy(p, t):
        to = lax.rem(mine + t, groups)
        return pltpu.make_async_remote_copy(
            src_ref=answer.at[p, to],
            dst_ref=result_lines(p),
            send_sem=back_send.at[p, t],
            recv_sem=back_recv.at[p, t],
            device_id={"mem": to},
        )

    def back_local(p):
        return pltpu.make_async_copy(answer.at[p, mine], result_lines(p), back_own.at[p])

    for t in range(1, groups):
        obs_copy(t).start()
    keep = pltpu.make_async_copy(obs.at[mine], obs_in.at[mine], obs_own)
    keep.start()

    for q in turns:
        load(q).wait()

        def turn(b, carry, q=q):
            row = pl.multiple_of(q * part_lines + b * 8, 8)
            for v in range(variables):
                block = raw[:, v, pl.ds(row, 8)]
                field[v, pl.ds(row + 1, 8)] = jnp.swapaxes(block, 0, 1)
            return carry

        lax.fori_loop(0, part_lines // 8, turn, 0)
        if q == parts - 1:
            for copy in halos:
                copy.start()
    for copy in halos:
        copy.wait()
    for place, outside in ((0, tile == 0), (lines + 1, tile == tiles - 1)):
        for v in range(variables):
            field[v, place] = jnp.where(outside, 0.0, field[v, place])

    lane = lax.broadcasted_iota(jnp.int32, (share, span), 1)

    def advance(p, to):
        def one_line(r, carry):
            line = to * device_lines + p * patch_lines + r
            here = [field[w, line + 1] for w in range(variables)]
            for v in range(variables):
                own = here[v]
                west = jnp.where(lane == 0, 0.0, pltpu.roll(own, 1, 1))
                east = jnp.where(lane == span - 1, 0.0, pltpu.roll(own, span - 1, 1))
                laplace = field[v, line + 2] + field[v, line] + east + west - 4.0 * own
                total = own + factor[v] * laplace
                for w in range(variables):
                    total += tendency[v, w] * here[w]
                outbox[to, p, v, r] = total
            return carry

        lax.fori_loop(0, patch_lines, one_line, 0)

    def forecast(p, carry):
        for t in order:
            advance(p, lax.rem(mine + t, groups))
            go_copy(p, t).start()
        advance(p, mine)
        go_local(p).start()
        return carry

    lax.fori_loop(0, per_device, forecast, 0)

    for t in range(1, groups):
        obs_copy(t).wait()
    keep.wait()

    slots = -(-groups // lanes_own) * LANES
    rows_i = lax.broadcasted_iota(jnp.int32, (members, members), 0)
    cols_i = lax.broadcasted_iota(jnp.int32, (members, members), 1)
    identity = jnp.where(rows_i == cols_i, 1.0, 0.0)
    cell = lax.broadcasted_iota(jnp.int32, (span, slots), 0)

    def analyse(p, carry):
        packs = []
        for first in range(0, groups, lanes_own):
            pack = obs_in[first, p]
            for s in range(first + 1, min(first + lanes_own, groups)):
                pack += obs_in[s, p]
            packs.append(pack)
        pack = jnp.concatenate(packs, axis=1)
        value, weight = pack[0:1], pack[1:2]
        column = pack[2:3].astype(jnp.int32)
        picked[...] = jnp.zeros_like(picked)
        for t in range(1, groups):
            go_copy(p, t).wait_recv()
        go_local(p).wait()

        def gather(c, carry):
            v, r = c // patch_lines, c % patch_lines
            block = inbox[p, :, v, r].reshape(members, span)
            mean = jnp.sum(block, axis=0, keepdims=True) * (1.0 / members)
            away = block - mean
            dev[c] = away
            wide = jnp.broadcast_to(mean, (16, span))
            centre[c] = wide[:8]
            parts = jnp.concatenate(split3(away) + split3(wide), axis=0)
            chosen = jnp.where(cell == column - c * span, 1.0, 0.0).astype(jnp.bfloat16)
            picked[...] += jnp.dot(parts, chosen, preferred_element_type=jnp.float32)
            return carry

        lax.fori_loop(0, chunks, gather, 0)
        seen = picked[0:members] + picked[members : 2 * members] + picked[2 * members : 3 * members]
        low = 3 * members
        middle_seen = picked[low : low + 8] + picked[low + 16 : low + 24] + picked[low + 32 : low + 40]
        innovation = value - middle_seen
        weighted = seen * weight
        gram = dot(weighted, seen, ((1,), (1,)))
        drive = jnp.sum(weighted * innovation[0:1], axis=1, keepdims=True)
        system = (members - 1.0) * identity + gram
        squares = jnp.sum(system * system, axis=1, keepdims=True)
        norm = jnp.sqrt(jnp.sum(squares, axis=0, keepdims=True))

        def sweep(i, pair):
            middle = 1.5 * identity - 0.5 * dot(pair[:, members:], pair[:, :members])
            return dot(middle, pair)

        start = jnp.concatenate([system / norm, identity], axis=1)
        pair = start
        for i in range(NS_ITERS):
            pair = sweep(i, pair)
        inverse = pair[:, members:]
        root = inverse / jnp.sqrt(norm)
        inner = jnp.sum(root * drive, axis=0, keepdims=True)
        offset = jnp.sum(root * inner, axis=1, keepdims=True)
        offset = jnp.sum(identity * offset, axis=0, keepdims=True)
        coeffs = offset + float(members - 1) ** 0.5 * root

        def mix(c, carry):
            v, r = c // patch_lines, c % patch_lines
            mixed = dot(coeffs, dev[c]) + centre[c, 0:1]
            answer[p, :, v, r] = mixed.reshape(groups, share, span)
            return carry

        lax.fori_loop(0, chunks, mix, 0)
        for t in order:
            back_copy(p, t).start()
        back_local(p).start()
        return carry

    lax.fori_loop(0, per_device, analyse, 0)

    def finish(p, carry):
        for t in range(1, groups):
            go_copy(p, t).wait_send()
        for t in range(1, groups):
            back_copy(p, t).wait()
        back_local(p).wait()
        return carry

    lax.fori_loop(0, per_device, finish, 0)


def turn_kernel(lines_first, members_out):
    for r in range(0, lines_first.shape[1], 8):
        members_out[:, 0, r : r + 8] = jnp.swapaxes(lines_first[0, r : r + 8], 0, 1)


def members_first(result):
    variables, lines, share, span = result.shape
    block = 64 if lines % 64 == 0 else 32
    return pl.pallas_call(
        turn_kernel,
        out_shape=jax.ShapeDtypeStruct((share, variables, lines, span), jnp.float32),
        grid=(variables, lines // block),
        in_specs=[pl.BlockSpec((1, block, share, span), lambda v, b: (v, b, 0, 0))],
        out_specs=pl.BlockSpec((share, 1, block, span), lambda v, b: (0, v, b, 0)),
    )(result)


def fused(
    prior_ensemble,
    spreading_factor,
    tendency_matrix,
    measured_data,
    inverse_error,
    assigned_subregion,
    measured_entry,
    taper_index,
    taper_factors,
):
    share, variables, lines, span = prior_ensemble.shape
    groups, tiles = lax.axis_size("mem"), lax.axis_size("dom")
    patch_lines = PATCH // span
    per_device = lines // groups // patch_lines
    per_tile = per_device * groups
    members = share * groups
    patch_ids = assigned_subregion.reshape(-1)
    obs_rows = patch_ids.shape[0]
    capacity = 2 * obs_rows // per_tile
    lanes_own = LANES // capacity
    levels = jnp.arange(taper_factors.shape[0], dtype=jnp.int32)
    taper = jnp.sum(
        jnp.where(taper_index.reshape(-1)[:, None] == levels[None], taper_factors[None], 0.0), axis=1
    )
    weight = inverse_error.reshape(-1) * taper
    number = jnp.arange(obs_rows, dtype=jnp.int32)
    rank = jnp.sum(
        ((patch_ids[None, :] == patch_ids[:, None]) & (number[None, :] < number[:, None])).astype(jnp.int32),
        axis=1,
    )
    slot = lax.rem(lax.axis_index("mem"), lanes_own) * capacity + rank
    nothing = jnp.zeros_like(weight)
    fields = jnp.stack(
        [measured_data.reshape(-1), weight, measured_entry.reshape(-1).astype(jnp.float32)]
        + [nothing] * 5
    )
    patches = jnp.arange(per_tile, dtype=jnp.int32)
    spread = jnp.where(patch_ids[None, None] == patches[:, None, None], fields[None], 0.0)
    places = (slot[:, None] == jnp.arange(LANES, dtype=jnp.int32)[None]).astype(jnp.float32)
    obs = jnp.dot(spread.reshape(per_tile * 8, obs_rows), places, precision=HIGH)
    obs = obs.reshape(groups, per_device, 8, LANES)
    chunks = variables * patch_lines
    slots = -(-groups // lanes_own) * LANES
    dma = pltpu.SemaphoreType.DMA
    result = pl.pallas_call(
        functools.partial(analysis_kernel, groups, tiles, per_device, patch_lines, lanes_own),
        out_shape=jax.ShapeDtypeStruct((variables, lines, share, span), jnp.float32),
        in_specs=[
            pl.BlockSpec(memory_space=pltpu.SMEM),
            pl.BlockSpec(memory_space=pltpu.SMEM),
            pl.BlockSpec(memory_space=pl.ANY),
            pl.BlockSpec(memory_space=pltpu.VMEM),
        ],
        out_specs=pl.BlockSpec(memory_space=pl.ANY),
        scratch_shapes=[
            pltpu.VMEM((share, variables, lines, span), jnp.float32),
            pltpu.VMEM((variables, lines + 2, share, span), jnp.float32),
            pltpu.VMEM((groups, per_device, variables, patch_lines, share, span), jnp.float32),
            pltpu.VMEM((per_device, groups, variables, patch_lines, share, span), jnp.float32),
            pltpu.VMEM((per_device, groups, variables, patch_lines, share, span), jnp.float32),
            pltpu.VMEM((groups, per_device, 8, LANES), jnp.float32),
            pltpu.VMEM((chunks, members, span), jnp.float32),
            pltpu.VMEM((chunks, 8, span), jnp.float32),
            pltpu.VMEM((3 * members + 48, slots), jnp.float32),
            dma((4,)), dma((2,)), dma((2,)), dma((groups,)), dma((groups,)), dma,
            dma((per_device, groups)), dma((per_device, groups)), dma((per_device,)),
            dma((per_device, groups)), dma((per_device, groups)), dma((per_device,)),
        ],
        compiler_params=pltpu.CompilerParams(
            collective_id=0, has_side_effects=True, vmem_limit_bytes=60 * 1024 * 1024
        ),
    )(spreading_factor, tendency_matrix, prior_ensemble, obs)
    return members_first(result)


def step(prior_ensemble, *rest):
    share, _, lines, span = prior_ensemble.shape
    groups, tiles = lax.axis_size("mem"), lax.axis_size("dom")
    whole_lines = PATCH % span == 0 and lines % (groups * (PATCH // span)) == 0
    obs_rows = rest[2].shape[-1]
    capacity = 2 * obs_rows * PATCH // (lines * span)
    if share % 8 == 0 and whole_lines and lines % 32 == 0 and tiles > 1 and groups > 1 and LANES % capacity == 0:
        return fused(prior_ensemble, *rest)
    return shards(prior_ensemble, *rest)


def solution(mesh):
    in_specs = (
        P("mem", None, "dom", None),
        P(),
        P(),
        P("dom", "mem"),
        P("dom", "mem"),
        P("dom", "mem", None),
        P("dom", "mem"),
        P("dom", "mem"),
        P(),
    )
    out_specs = P("mem", None, "dom", None)
    return jax.shard_map(step, mesh=mesh, in_specs=in_specs, out_specs=out_specs, check_vma=False)
```
